32 devices in a mesh: sx: 8 (over y, x, core), sy: 4 (over z).
Axes of the slice: x: 2, y: 2, z: 4, core: 2. Of those that a mesh axis runs over, the one named last changes fastest.
Arguments:
- coeffs: float32 [2, 8, 16, 4, 128, 128], P(None, 'sx', None, 'sy'), may hold values from -6 to 6
- deform: float32 [2, 4], replicated, may hold values from -0.08 to 0.08
Outputs:
- spectrum: float32 [2, 128, 512, 128], P(None, 'sx', 'sy')
The draws below stay inside these ranges and needn't reach their ends.
All inputs are finite; a program needn't handle non-finite values.
Results may differ from the reference program's by a relative error of at most 0.0014.
Values sent between devices are 32-bit elements; how exact they have to be, the bound alone decides.
A program may use at most 64 MiB of HBM per device.

```python
import math
import jax
import jax.numpy as jnp
import numpy as np
from jax import lax

NODES = 4
MODES = 4
RHS = 8
FBX = 16
FBY = 128
SBX = 8
SBY = 4


def block_scale(own_key, shape, cuts, low, largest):
    def one(dim, shards_of):
        draws = jax.random.uniform(jax.random.fold_in(jax.random.fold_in(own_key, 6), dim), (shards_of,), jnp.float32, low / len(cuts), largest / len(cuts))
        return jnp.repeat(jnp.exp(draws), shape[dim] // shards_of).reshape((-1,) + (1,) * (len(shape) - dim - 1))

    gain = one(*cuts[0])
    for cut in cuts[1:]:
        gain = gain * one(*cut)
    return gain


def bell_draw(key, extent, width, bound, cuts=(), kind=jnp.bfloat16):
    factor_of = block_scale(key, extent, cuts, -0.22, 0.18) if cuts else 1.0
    array = jax.random.normal(key, extent, jnp.float32) * width * factor_of
    return jnp.minimum(jnp.maximum(array, -bound), bound).astype(kind)


def setup_inputs(seed: int = 0) -> dict:
    keys = jax.random.split(jax.random.key(seed), 3)
    coeffs = bell_draw(keys[0], (2, SBX, FBX, SBY, FBY, RHS * NODES * NODES), 1.0, 6.0, ((1, 8), (3, 4)), jnp.float32)
    deform = jnp.clip(jax.random.uniform(keys[1], (2, MODES), jnp.float32, -0.08, 0.08), -0.08, 0.08)
    return {"coeffs": coeffs, "deform": deform}


two_pi = 2.0 * math.pi
step_scale = math.sqrt(0.5)

def cheb_nodes(count):
    return (1.0 - np.cos(np.pi * (2.0 * np.arange(count) + 1.0) / (2.0 * count))) / 2.0

def lagrange_table(count):
    nodes = cheb_nodes(count)
    table = np.ones((count, 2, count))
    for target_row in range(count):
        for sibling in range(2):
            spots = (sibling + nodes) / 2.0
            for other_node in range(count):
                if other_node != target_row:
                    table[target_row, sibling] = table[target_row, sibling] * (spots - nodes[other_node]) / (nodes[target_row] - nodes[other_node])
    return table

def rotation(first_pos, second_pos, first_freq, second_freq, deform, scales):
    first_grid = first_pos[:, :, None, None] + jnp.zeros_like(second_pos)[None, None, :, :]
    second_grid = second_pos[None, None, :, :] + jnp.zeros_like(first_pos)[:, :, None, None]
    harmonic = jnp.arange(1, deform.shape[1] + 1).astype(jnp.float32) * math.pi
    summed = (first_grid + second_grid)[..., None] * harmonic
    differ = (first_grid - second_grid)[..., None] * harmonic
    first_warp = first_grid + lax.optimization_barrier(jnp.sum(deform[0] * jnp.sin(summed), axis=-1))
    second_warp = second_grid + lax.optimization_barrier(jnp.sum(deform[1] * jnp.sin(differ), axis=-1))
    angles = scales[0] * (first_warp[..., None, None] * first_freq[:, None]) + scales[1] * (second_warp[..., None, None] * second_freq[None, :])
    return (jnp.cos(angles), jnp.sin(angles))

def orient(own_pos, other_pos, own_centre, other_centre, along, deform, scales):
    if along == 0:
        return rotation(own_pos, other_pos, own_centre, other_centre, deform, scales)
    return rotation(other_pos, own_pos, other_centre, own_centre, deform, scales)

def advance(children, parents, along, parent_count, other_boxes, other_count, parent_freq, freq_count, other_freq, other_fcount, deform, nodes, scales):
    other_pos = (other_boxes.astype(jnp.float32)[:, None] + nodes[None, :]) / other_count
    other_centre = (other_freq.astype(jnp.float32) + 0.5) / other_fcount
    parent_pos = (parents.astype(jnp.float32)[:, None] + nodes[None, :]) / parent_count
    pattern = 'au,rkuyvfg->rkayvfg' if along == 0 else 'bv,rxukvfg->rxukbfg'
    pieces = []
    for freq_child in range(2):
        centre = ((2 * parent_freq + freq_child).astype(jnp.float32) + 0.5) / (2 * freq_count)
        total_real = None
        total_imag = None
        for member, boxes, weights in children:
            child_pos = (boxes.astype(jnp.float32)[:, None] + nodes[None, :]) / (2 * parent_count)
            cosine, sine = orient(child_pos, other_pos, centre, other_centre, along, deform, scales)
            real_part = member[0] * cosine + member[1] * sine
            imag_part = member[1] * cosine - member[0] * sine
            mixed_real = jnp.einsum(pattern, weights, real_part, precision=lax.Precision.HIGHEST)
            mixed_imag = jnp.einsum(pattern, weights, imag_part, precision=lax.Precision.HIGHEST)
            if total_real is None:
                total_real, total_imag = (mixed_real, mixed_imag)
            else:
                total_real, total_imag = (total_real + mixed_real, total_imag + mixed_imag)
        cosine, sine = orient(parent_pos, other_pos, centre, other_centre, along, deform, scales)
        out_real = (total_real * cosine - total_imag * sine) * step_scale
        out_imag = (total_imag * cosine + total_real * sine) * step_scale
        pieces.append(jnp.stack([out_real, out_imag], axis=0))
    if along == 0:
        joined = jnp.stack(pieces, axis=7)
        dims = joined.shape
        return joined.reshape(dims[:6] + (dims[6] * 2, dims[8]))
    joined = jnp.stack(pieces, axis=8)
    dims = joined.shape
    return joined.reshape(dims[:7] + (dims[7] * 2,))

def local_levels(state, x_boxes, y_boxes, x_freq, x_count, y_freq, y_count, deform, nodes, lagrange, scales):
    x_bits = x_boxes.shape[0].bit_length() - 1
    y_bits = y_boxes.shape[0].bit_length() - 1
    pair_idx = jnp.arange(2).astype(jnp.int32)
    for depth in range(max(x_bits, y_bits)):
        if depth < x_bits:
            pairs = x_boxes.shape[0] // 2
            dims = state.shape
            split = state.reshape(dims[0], dims[1], pairs, 2, dims[3], dims[4], dims[5], dims[6], dims[7])
            parent_boxes = jnp.arange(pairs).astype(jnp.int32)
            children = [(split[:, :, :, 0], 2 * parent_boxes, lagrange[:, 0]), (split[:, :, :, 1], 2 * parent_boxes + 1, lagrange[:, 1])]
            state = advance(children, parent_boxes, 0, pairs, y_boxes, y_boxes.shape[0], x_freq, x_count, y_freq, y_count, deform, nodes, scales)
            x_freq = (2 * x_freq[:, None] + pair_idx[None, :]).reshape(-1)
            x_count = 2 * x_count
            x_boxes = parent_boxes
        if depth < y_bits:
            pairs = y_boxes.shape[0] // 2
            dims = state.shape
            split = state.reshape(dims[0], dims[1], dims[2], dims[3], pairs, 2, dims[5], dims[6], dims[7])
            parent_boxes = jnp.arange(pairs).astype(jnp.int32)
            children = [(split[:, :, :, :, :, 0], 2 * parent_boxes, lagrange[:, 0]), (split[:, :, :, :, :, 1], 2 * parent_boxes + 1, lagrange[:, 1])]
            state = advance(children, parent_boxes, 1, pairs, x_boxes, x_boxes.shape[0], y_freq, y_count, x_freq, x_count, deform, nodes, scales)
            y_freq = (2 * y_freq[:, None] + pair_idx[None, :]).reshape(-1)
            y_count = 2 * y_count
            y_boxes = parent_boxes
    return state

def reference(coeffs, deform):
    node_count = NODES
    right_sides = RHS
    space_x = coeffs.shape[1]
    freq_x = coeffs.shape[2]
    space_y = coeffs.shape[3]
    freq_y = coeffs.shape[4]
    old = coeffs.reshape(2, space_x, freq_x, space_y, freq_y, right_sides, node_count, node_count)
    old = jnp.transpose(old, (0, 5, 1, 6, 3, 7, 2, 4))
    nodes = jnp.asarray(cheb_nodes(node_count), dtype=jnp.float32)
    lagrange = jnp.asarray(lagrange_table(node_count), dtype=jnp.float32)
    scales = (two_pi * float(space_x * freq_x), two_pi * float(space_y * freq_y))

    def single(column):
        state = column[:, None]
        x_boxes = jnp.arange(space_x).astype(jnp.int32)
        y_boxes = jnp.arange(space_y).astype(jnp.int32)
        x_freq = jnp.arange(freq_x).astype(jnp.int32)
        y_freq = jnp.arange(freq_y).astype(jnp.int32)
        final = local_levels(state, x_boxes, y_boxes, x_freq, freq_x, y_freq, freq_y, deform, nodes, lagrange, scales)
        return final[:, 0, 0, :, 0, :, :, :]
    result = lax.map(single, jnp.moveaxis(old, 1, 0))
    result = jnp.moveaxis(result, 0, 1)
    result = jnp.transpose(result, (0, 4, 5, 1, 2, 3))
    dims = result.shape
    return result.reshape(2, dims[1], dims[2], right_sides * node_count * node_count)
```

```python
import functools
import math

import jax
import jax.numpy as jnp
import numpy as np
from jax import lax
from jax.experimental import pallas as pl
from jax.experimental.pallas import tpu as pltpu
from jax.sharding import PartitionSpec as P

NODES = 4
RHS = 8
ROWS = 8
MESH = pl.DeviceIdType.MESH


def cheb_nodes(count):
    return (1.0 - np.cos(np.pi * (2.0 * np.arange(count) + 1.0) / (2.0 * count))) / 2.0


def lagrange_table(count):
    nodes = cheb_nodes(count)
    table = np.ones((count, 2, count))
    for row in range(count):
        for sibling in range(2):
            spots = (sibling + nodes) / 2.0
            for other in range(count):
                if other != row:
                    table[row, sibling] *= (spots - nodes[other]) / (nodes[row] - nodes[other])
    return table


def mix_matrix(along, right_sides, count):
    table = lagrange_table(count)
    blocks = []
    for sibling in range(2):
        weights = table[:, sibling].T
        eye = np.eye(count)
        inner = np.kron(weights, eye) if along == 0 else np.kron(eye, weights)
        blocks.append(np.kron(np.eye(right_sides), inner))
    return (np.concatenate(blocks, axis=0) * math.sqrt(0.5)).astype(np.float32)


TAYLOR_SIN = [((-1.0) ** k) * (2.0 * math.pi) ** (2 * k + 1) / math.factorial(2 * k + 1) for k in range(8)]
TAYLOR_COS = [((-1.0) ** k) * (2.0 * math.pi) ** (2 * k) / math.factorial(2 * k) for k in range(8)]


def horner(coefs, u):
    acc = coefs[-1] * u + coefs[-2]
    for c in coefs[-3::-1]:
        acc = acc * u + c
    return acc


def turns(t):
    half = jnp.floor(2.0 * t + 0.5)
    rest = t - 0.5 * half
    parity = half - 2.0 * jnp.floor(0.5 * half)
    sign = 1.0 - 2.0 * parity
    u = rest * rest
    return sign * horner(TAYLOR_COS, u), sign * rest * horner(TAYLOR_SIN, u)


def split_index(value, by):
    return lax.div(value, by), lax.rem(value, by)


def plan_of(space_x, space_y):
    steps = []
    sx, sy, row = space_x, space_y, 0
    while sx > 1 or sy > 1:
        if sx > 1:
            steps.append((0, sx, sy, row))
            row += max(8, sx * sy)
            sx //= 2
        if sy > 1:
            steps.append((1, sx, sy, row))
            row += max(8, sx * sy)
            sy //= 2
    return steps, row


def kernel(
    dims,
    deform_ref,
    nodes_ref,
    mix_ref,
    coeffs_ref,
    out_ref,
    recv,
    twid,
    base1,
    base2,
    last1,
    last2,
    lhs,
    state,
    send_sem,
    recv_sem,
):
    space_x, space_y, local_x, local_y, rows, modes = dims
    steps, _ = plan_of(space_x, space_y)
    chunks_y = local_y // rows
    chunks = local_x * chunks_y
    boxes = space_x * space_y
    gain_x, gain_y = space_x, space_y
    mx = lax.axis_index("sx")
    my = lax.axis_index("sy")
    me = mx * space_y + my

    barrier = pltpu.get_barrier_semaphore()

    def peer_of(i):
        ox, oy = split_index(i, space_y)
        return lax.rem(mx + ox, space_x), lax.rem(my + oy, space_y)

    def greet(i, _):
        px, py = peer_of(i)
        pl.semaphore_signal(barrier, inc=1, device_id=(px, py), device_id_type=MESH)
        return 0

    lax.fori_loop(1, boxes, greet, 0)

    node_x = nodes_ref[0:1, :]
    node_y = nodes_ref[1:2, :]

    def warped(sx, sy, count):
        box = lax.broadcasted_iota(jnp.int32, (count, 128), 0)
        ax = (box // sy).astype(jnp.float32)
        ay = (box % sy).astype(jnp.float32)
        p1 = (ax + node_x) / sx
        p2 = (ay + node_y) / sy
        y1, y2 = 0.0, 0.0
        for m in range(modes):
            y1 = y1 + deform_ref[0, m] * turns((p1 + p2) * (0.5 * (m + 1)))[1]
            y2 = y2 + deform_ref[1, m] * turns((p1 - p2) * (0.5 * (m + 1)))[1]
        return p1 + y1, p2 + y2

    for along, sx, sy, row in steps[1:]:
        count = max(8, sx * sy)
        y1, y2 = warped(sx, sy, count)
        c, s = turns((y1 * (0.25 * sx)) if along == 0 else (y2 * (0.25 * sy)))
        twid[0, pl.ds(row, count), :] = c
        twid[1, pl.ds(row, count), :] = s

    y1, y2 = warped(space_x, space_y, boxes)
    for fx in range(local_x):
        for child in range(2):
            freq = (mx * local_x + fx).astype(jnp.float32) + (0.25 + 0.5 * child)
            c, s = turns(y1 * (freq * gain_x))
            base1[0, 2 * fx + child] = c
            base1[1, 2 * fx + child] = s
    twid[0, pl.ds(0, boxes), :] = y2

    def base_box(i, _):
        freq = lax.broadcasted_iota(jnp.int32, (local_y, 128), 0) + my * local_y
        warp = twid[0, pl.ds(i, 1), :]
        c, s = turns(warp * ((freq.astype(jnp.float32) + 0.5) * gain_y))
        base2[0, i] = c
        base2[1, i] = s
        return 0

    lax.fori_loop(0, boxes, base_box, 0)

    y1, y2 = warped(1, 1, 8)
    out_x = local_x * space_x
    freq = lax.broadcasted_iota(jnp.int32, (out_x, 128), 0) + mx * out_x
    c, s = turns(y1[0:1] * (freq.astype(jnp.float32) + 0.5))
    last1[0] = c
    last1[1] = s
    for child in range(space_y):
        freq = (lax.broadcasted_iota(jnp.int32, (local_y, 128), 0) + my * local_y) * space_y + child
        c, s = turns(y2[0:1] * (freq.astype(jnp.float32) + 0.5))
        last2[0, child] = c
        last2[1, child] = s

    pl.semaphore_wait(barrier, boxes - 1)

    def piece(k, px, py):
        fx, fy = split_index(k, chunks_y)
        start = pl.multiple_of(py * local_y + fy * rows, 8)
        return coeffs_ref.at[:, 0, px * local_x + fx, 0, pl.ds(start, rows), :]

    def send_chunk(k, _):
        def send(i, _):
            px, py = peer_of(i)
            pltpu.make_async_remote_copy(
                src_ref=piece(k, px, py),
                dst_ref=recv.at[k, me],
                send_sem=send_sem.at[k],
                recv_sem=recv_sem.at[k],
                device_id=(px, py),
                device_id_type=MESH,
            ).start()
            return 0

        lax.fori_loop(1, boxes, send, 0)
        pltpu.make_async_copy(piece(k, mx, my), recv.at[k, me], recv_sem.at[k]).start()
        return 0

    lax.fori_loop(0, chunks, send_chunk, 0)

    def rotate_into(slot, pair, sibling, size, re0, im0, re1, im1):
        lanes = pl.ds(128 * sibling, 128)
        base = pair * 4 * size
        lhs[slot, pl.ds(base, size), lanes] = re0
        lhs[slot, pl.ds(base + size, size), lanes] = im0
        lhs[slot, pl.ds(base + 2 * size, size), lanes] = re1
        lhs[slot, pl.ds(base + 3 * size, size), lanes] = im1

    def pair_of(along, sy, a1, a2):
        if along == 0:
            return (a1 // 2) * sy + a2, a1 % 2
        return a1 * (sy // 2) + a2 // 2, a2 % 2

    def compute(k, _):
        pltpu.make_async_copy(recv.at[k], recv.at[k], recv_sem.at[k]).wait()
        fx, fy = split_index(k, chunks_y)
        fy_rows = pl.ds(pl.multiple_of(fy * rows, 8), rows)
        size = rows
        for number, (along, sx, sy, row) in enumerate(steps):
            slot = number % 2
            for a1 in range(sx):
                for a2 in range(sy):
                    box = a1 * sy + a2
                    pair, sibling = pair_of(along, sy, a1, a2)
                    if number == 0:
                        re, im = recv[k, box, 0], recv[k, box, 1]
                        c, s = base2[0, box, fy_rows, :], base2[1, box, fy_rows, :]
                        re, im = re * c + im * s, im * c - re * s
                        c, s = base1[0, 2 * fx, pl.ds(box, 1), :], base1[1, 2 * fx, pl.ds(box, 1), :]
                        re0, im0 = re * c + im * s, im * c - re * s
                        c, s = base1[0, 2 * fx + 1, pl.ds(box, 1), :], base1[1, 2 * fx + 1, pl.ds(box, 1), :]
                        re1, im1 = re * c + im * s, im * c - re * s
                    else:
                        at = box * 2 * size
                        half = size // 2
                        re = jnp.concatenate(
                            [state[pl.ds(at, half), :], state[pl.ds(at + 2 * half, half), :]], axis=0
                        )
                        im = jnp.concatenate(
                            [state[pl.ds(at + half, half), :], state[pl.ds(at + 3 * half, half), :]], axis=0
                        )
                        c, s = twid[0, pl.ds(row + box, 1), :], twid[1, pl.ds(row + box, 1), :]
                        rc, rs, ic, js = re * c, re * s, im * c, im * s
                        re0, im0 = rc - js, ic + rs
                        re1, im1 = rc + js, ic - rs
                    rotate_into(slot, pair, sibling, size, re0, im0, re1, im1)
            state[...] = jnp.dot(
                lhs[slot], mix_ref[along], precision=lax.Precision.HIGHEST, preferred_element_type=jnp.float32
            )
            size *= 2
        total = len(steps)
        for code in range(1 << total):
            bits = [(code >> n) & 1 for n in range(total)]
            at = 0
            for n in range(total - 1):
                at += bits[n] * rows * (1 << n)
            half = rows * (1 << (total - 1))
            at += bits[total - 1] * 2 * half
            bx, by = 0, 0
            for n, (along, _, _, _) in enumerate(steps):
                if along == 0:
                    bx = 2 * bx + bits[n]
                else:
                    by = 2 * by + bits[n]
            re = state[pl.ds(at, rows), :]
            im = state[pl.ds(at + half, rows), :]
            first = fx * space_x + bx
            c1, s1 = last1[0, pl.ds(first, 1), :], last1[1, pl.ds(first, 1), :]
            c2, s2 = last2[0, by, fy_rows, :], last2[1, by, fy_rows, :]
            c = c1 * c2 - s1 * s2
            s = s1 * c2 + c1 * s2
            spots = pl.ds(fy * (rows * space_y) + by, rows, stride=space_y)
            out_ref[0, first, spots, :] = re * c - im * s
            out_ref[1, first, spots, :] = im * c + re * s
        return 0

    lax.fori_loop(0, chunks, compute, 0)

    def drain(k, _):
        sent = recv.at[k, pl.ds(0, boxes - 1)]
        pltpu.make_async_copy(sent, sent, send_sem.at[k]).wait()
        return 0

    lax.fori_loop(0, chunks, drain, 0)


def body(coeffs, deform):
    space_x, space_y = lax.axis_size("sx"), lax.axis_size("sy")
    _, _, freq_x, _, freq_y, lanes = coeffs.shape
    local_x, local_y = freq_x // space_x, freq_y // space_y
    rows = ROWS
    chunks = local_x * local_y // rows
    boxes = space_x * space_y
    out_x, out_y = local_x * space_x, local_y * space_y
    lane_ids = np.arange(lanes)
    table = cheb_nodes(NODES)
    nodes = jnp.asarray(
        np.stack([table[lane_ids // NODES % NODES], table[lane_ids % NODES]]), dtype=jnp.float32
    )
    right_sides = lanes // NODES**2
    mix = jnp.asarray(np.stack([mix_matrix(0, right_sides, NODES), mix_matrix(1, right_sides, NODES)]))
    _, twid_rows = plan_of(space_x, space_y)
    dims = (space_x, space_y, local_x, local_y, rows, deform.shape[1])
    vmem = pl.BlockSpec(memory_space=pltpu.VMEM)
    state_rows = boxes * 2 * rows
    f32 = jnp.float32
    return pl.pallas_call(
        functools.partial(kernel, dims),
        out_shape=jax.ShapeDtypeStruct((2, out_x, out_y, lanes), f32),
        in_specs=[
            pl.BlockSpec(memory_space=pltpu.SMEM),
            vmem,
            vmem,
            pl.BlockSpec(memory_space=pl.ANY),
        ],
        out_specs=vmem,
        scratch_shapes=[
            pltpu.VMEM((chunks, boxes, 2, rows, lanes), f32),
            pltpu.VMEM((2, twid_rows, lanes), f32),
            pltpu.VMEM((2, 2 * local_x, boxes, lanes), f32),
            pltpu.VMEM((2, boxes, local_y, lanes), f32),
            pltpu.VMEM((2, out_x, lanes), f32),
            pltpu.VMEM((2, space_y, local_y, lanes), f32),
            pltpu.VMEM((2, state_rows, 2 * lanes), f32),
            pltpu.VMEM((state_rows, lanes), f32),
            pltpu.SemaphoreType.DMA((chunks,)),
            pltpu.SemaphoreType.DMA((chunks,)),
        ],
        compiler_params=pltpu.CompilerParams(collective_id=0, has_side_effects=True),
        name="butterfly",
    )(deform, nodes, mix, coeffs)


def solution(mesh):
    placed = (P(None, "sx", None, "sy", None, None), P())
    return jax.shard_map(
        body, mesh=mesh, in_specs=placed, out_specs=P(None, "sx", "sy", None), check_vma=False
    )
```

```python
import functools
import math

import jax
import jax.numpy as jnp
import numpy as np
from jax import lax
from jax.experimental import pallas as pl
from jax.experimental.pallas import tpu as pltpu
from jax.sharding import PartitionSpec as P

NODES = 4
RHS = 8
ROWS = 8
MESH = pl.DeviceIdType.MESH


def cheb_nodes(count):
    return (1.0 - np.cos(np.pi * (2.0 * np.arange(count) + 1.0) / (2.0 * count))) / 2.0


def lagrange_table(count):
    nodes = cheb_nodes(count)
    table = np.ones((count, 2, count))
    for row in range(count):
        for sibling in range(2):
            spots = (sibling + nodes) / 2.0
            for other in range(count):
                if other != row:
                    table[row, sibling] *= (spots - nodes[other]) / (nodes[row] - nodes[other])
    return table


def mix_matrix(along, right_sides, count):
    table = lagrange_table(count)
    blocks = []
    for sibling in range(2):
        weights = table[:, sibling].T
        eye = np.eye(count)
        inner = np.kron(weights, eye) if along == 0 else np.kron(eye, weights)
        blocks.append(np.kron(np.eye(right_sides), inner))
    return (np.concatenate(blocks, axis=0) * math.sqrt(0.5)).astype(np.float32)


TAYLOR_SIN = [((-1.0) ** k) * (2.0 * math.pi) ** (2 * k + 1) / math.factorial(2 * k + 1) for k in range(8)]
TAYLOR_COS = [((-1.0) ** k) * (2.0 * math.pi) ** (2 * k) / math.factorial(2 * k) for k in range(8)]


def horner(coefs, u):
    acc = coefs[-1] * u + coefs[-2]
    for c in coefs[-3::-1]:
        acc = acc * u + c
    return acc


def turns(t):
    half = jnp.floor(2.0 * t + 0.5)
    rest = t - 0.5 * half
    parity = half - 2.0 * jnp.floor(0.5 * half)
    sign = 1.0 - 2.0 * parity
    u = rest * rest
    return sign * horner(TAYLOR_COS, u), sign * rest * horner(TAYLOR_SIN, u)


def split_index(value, by):
    return lax.div(value, by), lax.rem(value, by)


def plan_of(space_x, space_y):
    steps = []
    sx, sy, row = space_x, space_y, 0
    while sx > 1 or sy > 1:
        if sx > 1:
            steps.append((0, sx, sy, row))
            row += max(8, sx * sy)
            sx //= 2
        if sy > 1:
            steps.append((1, sx, sy, row))
            row += max(8, sx * sy)
            sy //= 2
    return steps, row


def kernel(
    dims,
    deform_ref,
    nodes_ref,
    mix_ref,
    coeffs_ref,
    out_ref,
    recv,
    twid,
    base1,
    base2,
    last1,
    last2,
    lhs_high,
    lhs_low,
    state,
    send_sem,
    recv_sem,
):
    space_x, space_y, local_x, local_y, rows, modes = dims
    steps, _ = plan_of(space_x, space_y)
    chunks_y = local_y // rows
    chunks = local_x * chunks_y
    boxes = space_x * space_y
    gain_x, gain_y = space_x, space_y
    mx = lax.axis_index("sx")
    my = lax.axis_index("sy")
    me = mx * space_y + my

    barrier = pltpu.get_barrier_semaphore()

    def peer_of(i):
        oy, ox = split_index(i, space_x)
        return lax.rem(mx + ox, space_x), lax.rem(my + space_y - oy, space_y)

    def greet(i, _):
        px, py = peer_of(i)
        pl.semaphore_signal(barrier, inc=1, device_id=(px, py), device_id_type=MESH)
        return 0

    lax.fori_loop(1, boxes, greet, 0)

    node_x = nodes_ref[0:1, :]
    node_y = nodes_ref[1:2, :]

    def warped(sx, sy, count):
        box = lax.broadcasted_iota(jnp.int32, (count, 128), 0)
        ax = (box // sy).astype(jnp.float32)
        ay = (box % sy).astype(jnp.float32)
        p1 = (ax + node_x) / sx
        p2 = (ay + node_y) / sy
        y1, y2 = 0.0, 0.0
        for m in range(modes):
            y1 = y1 + deform_ref[0, m] * turns((p1 + p2) * (0.5 * (m + 1)))[1]
            y2 = y2 + deform_ref[1, m] * turns((p1 - p2) * (0.5 * (m + 1)))[1]
        return p1 + y1, p2 + y2

    for along, sx, sy, row in steps[1:]:
        count = max(8, sx * sy)
        y1, y2 = warped(sx, sy, count)
        c, s = turns((y1 * (0.25 * sx)) if along == 0 else (y2 * (0.25 * sy)))
        twid[0, pl.ds(row, count), :] = c
        twid[1, pl.ds(row, count), :] = s

    y1, y2 = warped(space_x, space_y, boxes)
    for fx in range(local_x):
        for child in range(2):
            freq = (mx * local_x + fx).astype(jnp.float32) + (0.25 + 0.5 * child)
            c, s = turns(y1 * (freq * gain_x))
            base1[0, 2 * fx + child] = c
            base1[1, 2 * fx + child] = s
    twid[0, pl.ds(0, boxes), :] = y2

    def base_box(i, _):
        freq = lax.broadcasted_iota(jnp.int32, (local_y, 128), 0) + my * local_y
        warp = twid[0, pl.ds(i, 1), :]
        c, s = turns(warp * ((freq.astype(jnp.float32) + 0.5) * gain_y))
        base2[0, i] = c
        base2[1, i] = s
        return 0

    lax.fori_loop(0, boxes, base_box, 0)

    y1, y2 = warped(1, 1, 8)
    out_x = local_x * space_x
    freq = lax.broadcasted_iota(jnp.int32, (out_x, 128), 0) + mx * out_x
    c, s = turns(y1[0:1] * (freq.astype(jnp.float32) + 0.5))
    last1[0] = c
    last1[1] = s
    for child in range(space_y):
        freq = (lax.broadcasted_iota(jnp.int32, (local_y, 128), 0) + my * local_y) * space_y + child
        c, s = turns(y2[0:1] * (freq.astype(jnp.float32) + 0.5))
        last2[0, child] = c
        last2[1, child] = s

    pl.semaphore_wait(barrier, boxes - 1)

    def piece(k, px, py):
        fx, fy = split_index(k, chunks_y)
        start = pl.multiple_of(py * local_y + fy * rows, 8)
        return coeffs_ref.at[:, 0, px * local_x + fx, 0, pl.ds(start, rows), :]

    def send_chunk(k, _):
        def send(i, _):
            px, py = peer_of(boxes - i)
            pltpu.make_async_remote_copy(
                src_ref=piece(k, px, py),
                dst_ref=recv.at[k, me],
                send_sem=send_sem.at[k],
                recv_sem=recv_sem.at[k],
                device_id=(px, py),
                device_id_type=MESH,
            ).start()
            return 0

        lax.fori_loop(1, boxes, send, 0)
        pltpu.make_async_copy(piece(k, mx, my), recv.at[k, me], recv_sem.at[k]).start()
        return 0

    lax.fori_loop(0, chunks, send_chunk, 0)

    def rotate_into(slot, pair, sibling, size, re0, im0, re1, im1):
        spot = (slot, pl.ds(pair * 4 * size, 4 * size), pl.ds(128 * sibling, 128))
        whole = jnp.concatenate([re0, im0, re1, im1], axis=0)
        high = whole.astype(jnp.bfloat16)
        lhs_high[spot] = high
        lhs_low[spot] = (whole - high.astype(jnp.float32)).astype(jnp.bfloat16)

    def pair_of(along, sy, a1, a2):
        if along == 0:
            return (a1 // 2) * sy + a2, a1 % 2
        return a1 * (sy // 2) + a2 // 2, a2 % 2

    def compute(k, _):
        pltpu.make_async_copy(recv.at[k], recv.at[k], recv_sem.at[k]).wait()
        fx, fy = split_index(k, chunks_y)
        fy_rows = pl.ds(pl.multiple_of(fy * rows, 8), rows)
        size = rows
        for number, (along, sx, sy, row) in enumerate(steps):
            slot = number % 2
            for a1 in range(sx):
                for a2 in range(sy):
                    box = a1 * sy + a2
                    pair, sibling = pair_of(along, sy, a1, a2)
                    if number == 0:
                        re, im = recv[k, box, 0], recv[k, box, 1]
                        c, s = base2[0, box, fy_rows, :], base2[1, box, fy_rows, :]
                        re, im = re * c + im * s, im * c - re * s
                        c, s = base1[0, 2 * fx, pl.ds(box, 1), :], base1[1, 2 * fx, pl.ds(box, 1), :]
                        re0, im0 = re * c + im * s, im * c - re * s
                        c, s = base1[0, 2 * fx + 1, pl.ds(box, 1), :], base1[1, 2 * fx + 1, pl.ds(box, 1), :]
                        re1, im1 = re * c + im * s, im * c - re * s
                    else:
                        at = box * 2 * size
                        half = size // 2
                        re = jnp.concatenate(
                            [state[pl.ds(at, half), :], state[pl.ds(at + 2 * half, half), :]], axis=0
                        )
                        im = jnp.concatenate(
                            [state[pl.ds(at + half, half), :], state[pl.ds(at + 3 * half, half), :]], axis=0
                        )
                        c, s = twid[0, pl.ds(row + box, 1), :], twid[1, pl.ds(row + box, 1), :]
                        rc, rs, ic, js = re * c, re * s, im * c, im * s
                        re0, im0 = rc - js, ic + rs
                        re1, im1 = rc + js, ic - rs
                    rotate_into(slot, pair, sibling, size, re0, im0, re1, im1)
            by_high = jnp.dot(lhs_high[slot], mix_ref[along], preferred_element_type=jnp.float32)
            by_low = jnp.dot(lhs_low[slot], mix_ref[along, :, 0:128], preferred_element_type=jnp.float32)
            state[...] = by_high[:, 0:128] + (by_high[:, 128:256] + by_low)
            size *= 2
        total = len(steps)
        for code in range(1 << total):
            bits = [(code >> n) & 1 for n in range(total)]
            at = 0
            for n in range(total - 1):
                at += bits[n] * rows * (1 << n)
            half = rows * (1 << (total - 1))
            at += bits[total - 1] * 2 * half
            bx, by = 0, 0
            for n, (along, _, _, _) in enumerate(steps):
                if along == 0:
                    bx = 2 * bx + bits[n]
                else:
                    by = 2 * by + bits[n]
            re = state[pl.ds(at, rows), :]
            im = state[pl.ds(at + half, rows), :]
            first = fx * space_x + bx
            c1, s1 = last1[0, pl.ds(first, 1), :], last1[1, pl.ds(first, 1), :]
            c2, s2 = last2[0, by, fy_rows, :], last2[1, by, fy_rows, :]
            c = c1 * c2 - s1 * s2
            s = s1 * c2 + c1 * s2
            spots = pl.ds(fy * (rows * space_y) + by, rows, stride=space_y)
            out_ref[0, first, spots, :] = re * c - im * s
            out_ref[1, first, spots, :] = im * c + re * s
        return 0

    lax.fori_loop(0, chunks, compute, 0)

    def drain(k, _):
        sent = recv.at[k, pl.ds(0, boxes - 1)]
        pltpu.make_async_copy(sent, sent, send_sem.at[k]).wait()
        return 0

    lax.fori_loop(0, chunks, drain, 0)


def body(coeffs, deform):
    space_x, space_y = lax.axis_size("sx"), lax.axis_size("sy")
    _, _, freq_x, _, freq_y, lanes = coeffs.shape
    local_x, local_y = freq_x // space_x, freq_y // space_y
    rows = ROWS
    chunks = local_x * local_y // rows
    boxes = space_x * space_y
    out_x, out_y = local_x * space_x, local_y * space_y
    lane_ids = np.arange(lanes)
    table = cheb_nodes(NODES)
    nodes = jnp.asarray(
        np.stack([table[lane_ids // NODES % NODES], table[lane_ids % NODES]]), dtype=jnp.float32
    )
    right_sides = lanes // NODES**2
    mix = np.stack([mix_matrix(0, right_sides, NODES), mix_matrix(1, right_sides, NODES)])
    high = mix.astype(jnp.bfloat16)
    low = (mix - high.astype(np.float32)).astype(jnp.bfloat16)
    mix = jnp.asarray(np.concatenate([high, low], axis=2))
    _, twid_rows = plan_of(space_x, space_y)
    dims = (space_x, space_y, local_x, local_y, rows, deform.shape[1])
    vmem = pl.BlockSpec(memory_space=pltpu.VMEM)
    state_rows = boxes * 2 * rows
    f32 = jnp.float32
    return pl.pallas_call(
        functools.partial(kernel, dims),
        out_shape=pltpu.VMEM((2, out_x, out_y, lanes), f32),
        in_specs=[
            pl.BlockSpec(memory_space=pltpu.SMEM),
            vmem,
            vmem,
            pl.BlockSpec(memory_space=pl.ANY),
        ],
        out_specs=vmem,
        scratch_shapes=[
            pltpu.VMEM((chunks, boxes, 2, rows, lanes), f32),
            pltpu.VMEM((2, twid_rows, lanes), f32),
            pltpu.VMEM((2, 2 * local_x, boxes, lanes), f32),
            pltpu.VMEM((2, boxes, local_y, lanes), f32),
            pltpu.VMEM((2, out_x, lanes), f32),
            pltpu.VMEM((2, space_y, local_y, lanes), f32),
            pltpu.VMEM((2, state_rows, 2 * lanes), jnp.bfloat16),
            pltpu.VMEM((2, state_rows, 2 * lanes), jnp.bfloat16),
            pltpu.VMEM((state_rows, lanes), f32),
            pltpu.SemaphoreType.DMA((chunks,)),
            pltpu.SemaphoreType.DMA((chunks,)),
        ],
        compiler_params=pltpu.CompilerParams(collective_id=0, has_side_effects=True),
        name="butterfly",
    )(deform, nodes, mix, coeffs)


def solution(mesh):
    placed = (P(None, "sx", None, "sy", None, None), P())
    return jax.shard_map(
        body, mesh=mesh, in_specs=placed, out_specs=P(None, "sx", "sy", None), check_vma=False
    )
```

```python
import functools
import math

import jax
import jax.numpy as jnp
import numpy as np
from jax import lax
from jax.experimental import pallas as pl
from jax.experimental.pallas import tpu as pltpu
from jax.sharding import PartitionSpec as P

NODES = 4
RHS = 8
ROWS = 8
MESH = pl.DeviceIdType.MESH


def cheb_nodes(count):
    return (1.0 - np.cos(np.pi * (2.0 * np.arange(count) + 1.0) / (2.0 * count))) / 2.0


def lagrange_table(count):
    nodes = cheb_nodes(count)
    table = np.ones((count, 2, count))
    for row in range(count):
        for sibling in range(2):
            spots = (sibling + nodes) / 2.0
            for other in range(count):
                if other != row:
                    table[row, sibling] *= (spots - nodes[other]) / (nodes[row] - nodes[other])
    return table


def mix_matrix(along, right_sides, count):
    table = lagrange_table(count)
    blocks = []
    for sibling in range(2):
        weights = table[:, sibling].T
        eye = np.eye(count)
        inner = np.kron(weights, eye) if along == 0 else np.kron(eye, weights)
        blocks.append(np.kron(np.eye(right_sides), inner))
    return (np.concatenate(blocks, axis=0) * math.sqrt(0.5)).astype(np.float32)


TAYLOR_SIN = [((-1.0) ** k) * (2.0 * math.pi) ** (2 * k + 1) / math.factorial(2 * k + 1) for k in range(8)]
TAYLOR_COS = [((-1.0) ** k) * (2.0 * math.pi) ** (2 * k) / math.factorial(2 * k) for k in range(8)]


def horner(coefs, u):
    acc = coefs[-1] * u + coefs[-2]
    for c in coefs[-3::-1]:
        acc = acc * u + c
    return acc


def turns(t):
    half = jnp.floor(2.0 * t + 0.5)
    rest = t - 0.5 * half
    parity = half - 2.0 * jnp.floor(0.5 * half)
    sign = 1.0 - 2.0 * parity
    u = rest * rest
    return sign * horner(TAYLOR_COS, u), sign * rest * horner(TAYLOR_SIN, u)


def split_index(value, by):
    return lax.div(value, by), lax.rem(value, by)


def plan_of(space_x, space_y):
    steps = []
    sx, sy, row = space_x, space_y, 0
    while sx > 1 or sy > 1:
        if sx > 1:
            steps.append((0, sx, sy, row))
            row += max(8, sx * sy)
            sx //= 2
        if sy > 1:
            steps.append((1, sx, sy, row))
            row += max(8, sx * sy)
            sy //= 2
    return steps, row


def kernel(
    dims,
    deform_hbm,
    mix_hbm,
    coeffs_ref,
    out_ref,
    recv,
    twid,
    base1,
    base2,
    last1,
    last2,
    lhs_high,
    lhs_low,
    state,
    send_sem,
    recv_sem,
    deform_ref,
    mix_ref,
    deform_sem,
    mix_sem,
    plane_sem,
):
    space_x, space_y, local_x, local_y, rows, modes = dims
    steps, _ = plan_of(space_x, space_y)
    chunks_y = local_y // rows
    chunks = local_x * chunks_y
    boxes = space_x * space_y
    gain_x, gain_y = space_x, space_y
    mx = lax.axis_index("sx")
    my = lax.axis_index("sy")
    me = mx * space_y + my

    barrier = pltpu.get_barrier_semaphore()

    for o in range(1, space_y):
        pl.semaphore_signal(
            barrier, inc=1, device_id=(mx, lax.rem(my + o, space_y)), device_id_type=MESH
        )
    for o in range(1, space_x):
        pl.semaphore_signal(
            barrier, inc=1, device_id=(lax.rem(mx + o, space_x), my), device_id_type=MESH
        )
    fetch_mix = pltpu.make_async_copy(mix_hbm, mix_ref, mix_sem)
    fetch_mix.start()
    fetch_deform = pltpu.make_async_copy(deform_hbm, deform_ref, deform_sem)
    fetch_deform.start()
    fetch_deform.wait()

    lane = lax.broadcasted_iota(jnp.int32, (1, 128), 1)
    spots = [float(q) for q in cheb_nodes(NODES)]

    def node_of(index):
        node = jnp.full((1, 128), spots[0], jnp.float32)
        for t in range(1, NODES):
            node = jnp.where(index == t, spots[t], node)
        return node

    node_x = node_of(lane // NODES % NODES)
    node_y = node_of(lane % NODES)

    def warped(sx, sy, count):
        box = lax.broadcasted_iota(jnp.int32, (count, 128), 0)
        ax = (box // sy).astype(jnp.float32)
        ay = (box % sy).astype(jnp.float32)
        p1 = (ax + node_x) / sx
        p2 = (ay + node_y) / sy
        y1, y2 = 0.0, 0.0
        for m in range(modes):
            y1 = y1 + deform_ref[0, m] * turns((p1 + p2) * (0.5 * (m + 1)))[1]
            y2 = y2 + deform_ref[1, m] * turns((p1 - p2) * (0.5 * (m + 1)))[1]
        return p1 + y1, p2 + y2

    for along, sx, sy, row in steps[1:]:
        count = max(8, sx * sy)
        y1, y2 = warped(sx, sy, count)
        c, s = turns((y1 * (0.25 * sx)) if along == 0 else (y2 * (0.25 * sy)))
        twid[0, pl.ds(row, count), :] = c
        twid[1, pl.ds(row, count), :] = s

    y1, y2 = warped(space_x, space_y, boxes)
    for fx in range(local_x):
        for child in range(2):
            freq = (mx * local_x + fx).astype(jnp.float32) + (0.25 + 0.5 * child)
            c, s = turns(y1 * (freq * gain_x))
            base1[0, 2 * fx + child] = c
            base1[1, 2 * fx + child] = s
    twid[0, pl.ds(0, boxes), :] = y2

    def base_box(i, _):
        freq = lax.broadcasted_iota(jnp.int32, (local_y, 128), 0) + my * local_y
        warp = twid[0, pl.ds(i, 1), :]
        c, s = turns(warp * ((freq.astype(jnp.float32) + 0.5) * gain_y))
        base2[0, i] = c
        base2[1, i] = s
        return 0

    lax.fori_loop(0, boxes, base_box, 0)

    y1, y2 = warped(1, 1, 8)
    out_x = local_x * space_x
    freq = lax.broadcasted_iota(jnp.int32, (out_x, 128), 0) + mx * out_x
    c, s = turns(y1[0:1] * (freq.astype(jnp.float32) + 0.5))
    last1[0] = c
    last1[1] = s
    for child in range(space_y):
        freq = (lax.broadcasted_iota(jnp.int32, (local_y, 128), 0) + my * local_y) * space_y + child
        c, s = turns(y2[0:1] * (freq.astype(jnp.float32) + 0.5))
        last2[0, child] = c
        last2[1, child] = s

    def piece(k, px, py):
        fx, fy = split_index(k, chunks_y)
        start = pl.multiple_of(py * local_y + fy * rows, 8)
        return coeffs_ref.at[:, 0, px * local_x + fx, 0, pl.ds(start, rows), :]

    def send(k, px, py):
        pltpu.make_async_remote_copy(
            src_ref=piece(k, px, py),
            dst_ref=recv.at[k, me],
            send_sem=send_sem.at[k],
            recv_sem=recv_sem.at[k],
            device_id=(px, py),
            device_id_type=MESH,
        ).start()

    pl.semaphore_wait(barrier, space_x + space_y - 2)
    for o in range(1, space_x):
        pl.semaphore_signal(
            plane_sem, inc=1, device_id=(lax.rem(mx + o, space_x), my), device_id_type=MESH
        )

    def send_line(k, _):
        for o in range(1, space_y):
            send(k, mx, lax.rem(my + o, space_y))
        return 0

    lax.fori_loop(0, chunks, send_line, 0)
    pl.semaphore_wait(plane_sem, space_x - 1)

    def send_chunk(k, _):
        def send_one(i, _):
            oy, ox = split_index(i, space_x - 1)
            send(k, lax.rem(mx + 1 + ox, space_x), lax.rem(my + 1 + oy, space_y))
            return 0

        lax.fori_loop(0, boxes - space_y, send_one, 0)
        pltpu.make_async_copy(piece(k, mx, my), recv.at[k, me], recv_sem.at[k]).start()
        return 0

    lax.fori_loop(0, chunks, send_chunk, 0)
    fetch_mix.wait()

    def rotate_into(slot, pair, sibling, size, re0, im0, re1, im1):
        spot = (slot, pl.ds(pair * 4 * size, 4 * size), pl.ds(128 * sibling, 128))
        whole = jnp.concatenate([re0, im0, re1, im1], axis=0)
        high = whole.astype(jnp.bfloat16)
        lhs_high[spot] = high
        lhs_low[spot] = (whole - high.astype(jnp.float32)).astype(jnp.bfloat16)

    def pair_of(along, sy, a1, a2):
        if along == 0:
            return (a1 // 2) * sy + a2, a1 % 2
        return a1 * (sy // 2) + a2 // 2, a2 % 2

    def compute(k, _):
        pltpu.make_async_copy(recv.at[k], recv.at[k], recv_sem.at[k]).wait()
        fx, fy = split_index(k, chunks_y)
        fy_rows = pl.ds(pl.multiple_of(fy * rows, 8), rows)
        size = rows
        for number, (along, sx, sy, row) in enumerate(steps):
            slot = number % 2
            for a1 in range(sx):
                for a2 in range(sy):
                    box = a1 * sy + a2
                    pair, sibling = pair_of(along, sy, a1, a2)
                    if number == 0:
                        re, im = recv[k, box, 0], recv[k, box, 1]
                        c, s = base2[0, box, fy_rows, :], base2[1, box, fy_rows, :]
                        re, im = re * c + im * s, im * c - re * s
                        c, s = base1[0, 2 * fx, pl.ds(box, 1), :], base1[1, 2 * fx, pl.ds(box, 1), :]
                        re0, im0 = re * c + im * s, im * c - re * s
                        c, s = base1[0, 2 * fx + 1, pl.ds(box, 1), :], base1[1, 2 * fx + 1, pl.ds(box, 1), :]
                        re1, im1 = re * c + im * s, im * c - re * s
                    else:
                        at = box * 2 * size
                        half = size // 2
                        re = jnp.concatenate(
                            [state[pl.ds(at, half), :], state[pl.ds(at + 2 * half, half), :]], axis=0
                        )
                        im = jnp.concatenate(
                            [state[pl.ds(at + half, half), :], state[pl.ds(at + 3 * half, half), :]], axis=0
                        )
                        c, s = twid[0, pl.ds(row + box, 1), :], twid[1, pl.ds(row + box, 1), :]
                        rc, rs, ic, js = re * c, re * s, im * c, im * s
                        re0, im0 = rc - js, ic + rs
                        re1, im1 = rc + js, ic - rs
                    rotate_into(slot, pair, sibling, size, re0, im0, re1, im1)
            by_high = jnp.dot(lhs_high[slot], mix_ref[along], preferred_element_type=jnp.float32)
            by_low = jnp.dot(lhs_low[slot], mix_ref[along, :, 0:128], preferred_element_type=jnp.float32)
            state[...] = by_high[:, 0:128] + (by_high[:, 128:256] + by_low)
            size *= 2
        total = len(steps)
        for code in range(1 << total):
            bits = [(code >> n) & 1 for n in range(total)]
            at = 0
            for n in range(total - 1):
                at += bits[n] * rows * (1 << n)
            half = rows * (1 << (total - 1))
            at += bits[total - 1] * 2 * half
            bx, by = 0, 0
            for n, (along, _, _, _) in enumerate(steps):
                if along == 0:
                    bx = 2 * bx + bits[n]
                else:
                    by = 2 * by + bits[n]
            re = state[pl.ds(at, rows), :]
            im = state[pl.ds(at + half, rows), :]
            first = fx * space_x + bx
            c1, s1 = last1[0, pl.ds(first, 1), :], last1[1, pl.ds(first, 1), :]
            c2, s2 = last2[0, by, fy_rows, :], last2[1, by, fy_rows, :]
            c = c1 * c2 - s1 * s2
            s = s1 * c2 + c1 * s2
            spots = pl.ds(fy * (rows * space_y) + by, rows, stride=space_y)
            out_ref[0, first, spots, :] = re * c - im * s
            out_ref[1, first, spots, :] = im * c + re * s
        return 0

    lax.fori_loop(0, chunks, compute, 0)

    def drain(k, _):
        sent = recv.at[k, pl.ds(0, boxes - 1)]
        pltpu.make_async_copy(sent, sent, send_sem.at[k]).wait()
        return 0

    lax.fori_loop(0, chunks, drain, 0)


def body(coeffs, deform):
    space_x, space_y = lax.axis_size("sx"), lax.axis_size("sy")
    _, _, freq_x, _, freq_y, lanes = coeffs.shape
    local_x, local_y = freq_x // space_x, freq_y // space_y
    rows = ROWS
    chunks = local_x * local_y // rows
    boxes = space_x * space_y
    out_x, out_y = local_x * space_x, local_y * space_y
    right_sides = lanes // NODES**2
    mix = np.stack([mix_matrix(0, right_sides, NODES), mix_matrix(1, right_sides, NODES)])
    high = mix.astype(jnp.bfloat16)
    low = (mix - high.astype(np.float32)).astype(jnp.bfloat16)
    mix = jnp.asarray(np.concatenate([high, low], axis=2))
    _, twid_rows = plan_of(space_x, space_y)
    dims = (space_x, space_y, local_x, local_y, rows, deform.shape[1])
    vmem = pl.BlockSpec(memory_space=pltpu.VMEM)
    state_rows = boxes * 2 * rows
    f32 = jnp.float32
    return pl.pallas_call(
        functools.partial(kernel, dims),
        out_shape=pltpu.VMEM((2, out_x, out_y, lanes), f32),
        in_specs=[
            pl.BlockSpec(memory_space=pl.ANY),
            pl.BlockSpec(memory_space=pl.ANY),
            pl.BlockSpec(memory_space=pl.ANY),
        ],
        out_specs=vmem,
        scratch_shapes=[
            pltpu.VMEM((chunks, boxes, 2, rows, lanes), f32),
            pltpu.VMEM((2, twid_rows, lanes), f32),
            pltpu.VMEM((2, 2 * local_x, boxes, lanes), f32),
            pltpu.VMEM((2, boxes, local_y, lanes), f32),
            pltpu.VMEM((2, out_x, lanes), f32),
            pltpu.VMEM((2, space_y, local_y, lanes), f32),
            pltpu.VMEM((2, state_rows, 2 * lanes), jnp.bfloat16),
            pltpu.VMEM((2, state_rows, 2 * lanes), jnp.bfloat16),
            pltpu.VMEM((state_rows, lanes), f32),
            pltpu.SemaphoreType.DMA((chunks,)),
            pltpu.SemaphoreType.DMA((chunks,)),
            pltpu.SMEM(deform.shape, f32),
            pltpu.VMEM(mix.shape, mix.dtype),
            pltpu.SemaphoreType.DMA,
            pltpu.SemaphoreType.DMA,
            pltpu.SemaphoreType.REGULAR,
        ],
        compiler_params=pltpu.CompilerParams(collective_id=0, has_side_effects=True),
        name="butterfly",
    )(deform, mix, coeffs)


def solution(mesh):
    placed = (P(None, "sx", None, "sy", None, None), P())
    return jax.shard_map(
        body, mesh=mesh, in_specs=placed, out_specs=P(None, "sx", "sy", None), check_vma=False
    )
```
